32 devices in a mesh: expert: 8 (over z, y), layer: 4 (over x, core).
Axes of the slice: x: 2, y: 2, z: 4, core: 2. Of those that a mesh axis runs over, the one named last changes fastest.
Arguments:
- gradient: bfloat16 [32, 16, 1536], P(('layer', 'expert')), parts along dimension 0, may hold values from -80 to 80
- prior_stat: float32 [32, 8], P('layer'), parts along dimension 0, may hold values from -600 to 600, as said below
Outputs:
- update: bfloat16 [32, 16, 1536], P(('layer', 'expert')), parts along dimension 0
- statistic: float32 [32, 8], P('layer'), parts along dimension 0
The draws below stay inside these ranges and needn't reach their ends.
There are 4 independent parts, one for each index of `layer`. The reference program is written for one: setup_inputs(seed, part) draws one part's arguments, and reference() takes and returns one part's arrays. A program takes and returns all parts, laid end to end along the dimension named above; each array names one. Nothing has to cross between parts.
Inputs may be any that keep to these rules, and one draw needn't show every extreme that they name: `prior_stat`: symmetric positive definite.
All inputs are finite; a program needn't handle non-finite values.
Results may differ from the reference program's by a relative error of at most 0.001.
The reference program's roundings to bfloat16 on the way count: a program that leaves them out, or rounds other values in their place, can miss the bound.
Values may be sent and summed in bfloat16 or wider, within the bound.
A program may use at most 64 MiB of HBM per device.

```python
import jax
import jax.numpy as jnp
from jax import lax

F = 1536
ITERS = 5
EXPERTS = 8
D_SLAB = 16


def log_uniform(key, shape, low, high):
    return jnp.exp(jax.random.uniform(key, shape, jnp.float32, jnp.log(low), jnp.log(high)))


def draw_gradient(key, part):
    keys = jax.random.split(jax.random.fold_in(key, 11), 6)
    positions = jnp.arange(D_SLAB, dtype=jnp.float32) / max(D_SLAB - 1, 1)
    depth = 3.0 ** positions * log_uniform(keys[0], (D_SLAB,), 1.0, 2.0)
    column = log_uniform(keys[1], (F,), 0.3, 3.0)
    shared = jnp.clip(jax.random.normal(keys[2], (D_SLAB, F), jnp.float32), -4.0, 4.0)
    expert_scale = log_uniform(keys[3], (EXPERTS,), 0.56, 1.78)
    weight = jax.random.uniform(keys[4], (EXPERTS,), jnp.float32, -0.5, 0.5)
    noise = jnp.clip(jax.random.normal(keys[5], (EXPERTS, D_SLAB, F), jnp.float32), -4.0, 4.0)
    values = noise + weight[:, None, None] * shared[None]
    values = 0.25 * expert_scale[:, None, None] * depth[None, :, None] * column[None, None, :] * values
    return values.astype(jnp.bfloat16)


def draw_prior_stat(key, part):
    keys = jax.random.split(jax.random.fold_in(key, 23), 4)
    columns = 4 * EXPERTS
    scales = log_uniform(keys[0], (EXPERTS,), 0.56, 1.78)
    weight = jax.random.uniform(keys[1], (EXPERTS,), jnp.float32, -0.5, 0.5)
    noise = jnp.clip(jax.random.normal(keys[2], (EXPERTS, columns), jnp.float32), -4.0, 4.0)
    shared = jnp.clip(jax.random.normal(keys[3], (columns,), jnp.float32), -4.0, 4.0)
    basis = scales[:, None] * (noise + weight[:, None] * shared[None, :])
    product = jnp.dot(basis, basis.T, precision=lax.Precision.HIGHEST) / columns
    return product + 0.1 * jnp.diag(scales * scales)


def setup_inputs(seed: int = 0, part: int = 0) -> dict:
    splits = jax.random.split(jax.random.key(seed), 3)
    part_keys = jax.random.split(jax.random.fold_in(splits[2], part), 3)
    return {
        "gradient": draw_gradient(jax.random.fold_in(jax.random.fold_in(splits[2], part), 71), part),
        "prior_stat": draw_prior_stat(jax.random.fold_in(jax.random.fold_in(splits[2], part), 71), part),
    }


ridge_rate = 0.001
energy_floor = 1e-06

def matmul_high(left, right):
    return jnp.dot(left, right, precision=lax.Precision.HIGHEST, preferred_element_type=jnp.float32)

def inverse_root(statistic):
    count_rows = statistic.shape[0]
    identity = jnp.eye(count_rows, dtype=jnp.float32)
    ridge_term = ridge_rate * jnp.trace(statistic) / count_rows
    shifted = statistic + ridge_term * identity
    start_scale = 2.5 / jnp.sqrt(jnp.sum(shifted * shifted))
    matrix = start_scale * shifted
    root = start_scale ** 0.25 * identity
    for repeat in range(ITERS):
        factor = 1.25 * identity - 0.25 * matrix
        root = matmul_high(root, factor)
        square = matmul_high(factor, factor)
        matrix = matmul_high(matmul_high(square, square), matrix)
    return root

def reference(gradient, prior_stat):
    experts = gradient.shape[0]
    flattened = gradient.reshape(experts, -1)
    entries = flattened.shape[1]
    raw_gram = jnp.dot(flattened, flattened.T, preferred_element_type=jnp.float32)
    gram_mean = raw_gram / entries
    statistic = prior_stat + gram_mean
    root_bf = inverse_root(statistic).astype(jnp.bfloat16)
    products = jnp.dot(root_bf, flattened, preferred_element_type=jnp.float32)
    mixed_bf = products.astype(jnp.bfloat16)
    update_energy = jnp.sum(products * products) / (experts * entries)
    grad_energy = jnp.trace(gram_mean) / experts
    graft = jnp.sqrt((grad_energy + energy_floor) / (update_energy + energy_floor))
    fenced = lax.optimization_barrier(mixed_bf)
    update = (graft * fenced.astype(jnp.float32)).astype(jnp.bfloat16)
    return (update.reshape(gradient.shape), statistic)
```

```python
import functools

import jax
import jax.numpy as jnp
from jax import lax
from jax.experimental import pallas as pl
from jax.experimental.pallas import tpu as pltpu
from jax.sharding import PartitionSpec as P

ITERS = 5
ridge_rate = 0.001
energy_floor = 1e-06
LANES = 128
VMEM_BUDGET = 16 * 1024 * 1024


def matmul_high(left, right):
    return jnp.dot(left, right, precision=lax.Precision.HIGHEST, preferred_element_type=jnp.float32)


def inverse_root(statistic):
    count_rows = statistic.shape[0]
    identity = jnp.eye(count_rows, dtype=jnp.float32)
    ridge_term = ridge_rate * jnp.trace(statistic) / count_rows
    shifted = statistic + ridge_term * identity
    start_scale = 2.5 / jnp.sqrt(jnp.sum(shifted * shifted))
    matrix = start_scale * shifted
    root = start_scale**0.25 * identity
    for repeat in range(ITERS):
        factor = 1.25 * identity - 0.25 * matrix
        root = matmul_high(root, factor)
        square = matmul_high(factor, factor)
        matrix = matmul_high(matmul_high(square, square), matrix)
    return root


def apply_graft(mixed_bf, graft):
    fenced = lax.optimization_barrier(mixed_bf)
    return (graft * fenced.astype(jnp.float32)).astype(jnp.bfloat16)


def slice_grams(pieces):
    grams = jnp.einsum("eqrf,gqrf->eqrg", pieces, pieces, preferred_element_type=jnp.float32)
    return (pieces, grams)


def wide_body(gradient, prior_stat):
    experts = prior_stat.shape[0]
    owners = lax.axis_size("expert")
    local_experts = gradient.shape[0]
    slab_rows = gradient.shape[1]
    width = gradient.shape[2]
    entry_count = slab_rows * width
    slice_rows = slab_rows // owners
    blocked = gradient.reshape(local_experts, owners, slice_rows, width)
    regrouped, row_grams = slice_grams(
        lax.all_to_all(blocked, "expert", split_axis=1, concat_axis=0, tiled=True)
    )
    summed = lax.psum(jnp.sum(row_grams, axis=(1, 2)), "expert")
    gram_mean = summed / entry_count
    statistic = prior_stat + gram_mean
    root_bf = inverse_root(statistic).astype(jnp.bfloat16)
    flattened = regrouped.reshape(experts, -1)
    products = jnp.dot(root_bf, flattened, preferred_element_type=jnp.float32)
    mixed_bf = products.astype(jnp.bfloat16).reshape(experts, slice_rows, width)
    root_wide = root_bf.astype(jnp.float32)
    update_energy = jnp.sum(matmul_high(root_wide, gram_mean) * root_wide) / experts
    grad_energy = jnp.trace(gram_mean) / experts
    graft = jnp.sqrt((grad_energy + energy_floor) / (update_energy + energy_floor))
    grafted = apply_graft(mixed_bf, graft)
    update = lax.all_to_all(grafted, "expert", split_axis=0, concat_axis=1, tiled=True)
    return (update, statistic)


def splat_rows(columns, keep):
    for m, column in enumerate(columns):
        keep[m] = column


def entry(keep, k, m):
    return jnp.broadcast_to(keep[m, k : k + 1, :], keep.shape[1:])


def times(left, keep):
    size = len(left)
    out = []
    for m in range(size):
        terms = [left[k] * entry(keep, k, m) for k in range(size)]
        while len(terms) > 1:
            terms = [terms[i] + terms[i + 1] if i + 1 < len(terms) else terms[i] for i in range(0, len(terms), 2)]
        out.append(terms[0])
    return out


def total(tiles):
    acc = tiles[0]
    for tile in tiles[1:]:
        acc = acc + tile
    return jnp.broadcast_to(jnp.sum(acc, axis=0, keepdims=True), acc.shape)


def kernel(
    owners, gradient_ref, prior_ref, update_ref, statistic_ref, held, keep_gram, keep_matrix, keep_factor, keep_square,
    local_sem, send_sem, recv_sem,
):
    me = lax.axis_index("expert")
    experts = owners
    slab_rows, width = held.shape[1:]
    rows = experts * slab_rows

    local = pltpu.make_async_copy(gradient_ref.at[0], held.at[me], local_sem)
    local.start()
    barrier = pltpu.get_barrier_semaphore()
    for step in range(1, owners):
        peer = lax.rem(me + step, owners)
        pl.semaphore_signal(barrier, inc=1, device_id={"expert": peer}, device_id_type=pl.DeviceIdType.MESH)
    pl.semaphore_wait(barrier, owners - 1)
    copies = []
    for step in range(1, owners):
        peer = lax.rem(me + step, owners)
        copy = pltpu.make_async_remote_copy(
            src_ref=gradient_ref.at[0],
            dst_ref=held.at[me],
            send_sem=send_sem.at[step],
            recv_sem=recv_sem.at[step],
            device_id={"expert": peer},
            device_id_type=pl.DeviceIdType.MESH,
        )
        copy.start()
        copies.append(copy)

    tile = (experts, LANES)
    row = lax.broadcasted_iota(jnp.int32, tile, 0)
    lane = lax.broadcasted_iota(jnp.int32, tile, 1)
    unit = [jnp.where(row == k, 1.0, 0.0).astype(jnp.float32) for k in range(experts)]
    prior_wide = [jnp.broadcast_to(prior_ref[:, k : k + 1], tile) for k in range(experts)]

    local.wait()
    for copy in copies:
        copy.wait()

    flat = held[...].reshape(rows, width)
    full = lax.dot_general(flat, flat, (((1,), (1,)), ((), ())), preferred_element_type=jnp.float32)
    own = lax.broadcasted_iota(jnp.int32, (rows, rows), 0) % slab_rows
    other = lax.broadcasted_iota(jnp.int32, (rows, rows), 1) % slab_rows
    diagonal = jnp.where(own == other, full, 0.0)
    paired = jnp.sum(diagonal.reshape(experts, slab_rows, rows), axis=1)
    column_of = lax.broadcasted_iota(jnp.int32, (experts, rows), 1) // slab_rows
    gram_mean = [
        jnp.broadcast_to(
            jnp.sum(jnp.where(column_of == k, paired, 0.0), axis=1, keepdims=True) / (slab_rows * width), tile
        )
        for k in range(experts)
    ]
    splat_rows(gram_mean, keep_gram)
    statistic = [prior_wide[k] + gram_mean[k] for k in range(experts)]
    shown = statistic[0]
    for k in range(1, experts):
        shown = jnp.where(lane == k, statistic[k], shown)
    statistic_ref[...] = shown[:, :experts]

    ridge_term = ridge_rate * total([unit[k] * statistic[k] for k in range(experts)]) / experts
    shifted = [statistic[k] + ridge_term * unit[k] for k in range(experts)]
    start_scale = 2.5 / jnp.sqrt(total([s * s for s in shifted]))
    matrix = [start_scale * s for s in shifted]
    start_root = jnp.sqrt(jnp.sqrt(start_scale))
    root = [start_root * u for u in unit]
    for repeat in range(ITERS):
        factor = [1.25 * unit[k] - 0.25 * matrix[k] for k in range(experts)]
        splat_rows(factor, keep_factor)
        if repeat == 0:
            root = [start_root * f for f in factor]
        else:
            root = times(root, keep_factor)
        if repeat < ITERS - 1:
            splat_rows(matrix, keep_matrix)
            square = times(factor, keep_factor)
            splat_rows(square, keep_square)
            matrix = times(times(square, keep_square), keep_matrix)

    root_wide = [r.astype(jnp.bfloat16).astype(jnp.float32) for r in root]
    splat_rows(root_wide, keep_factor)
    mine = [jnp.broadcast_to(keep_factor[g, pl.ds(me, 1), :], tile)[:1] for g in range(experts)]
    spread = times(root_wide, keep_gram)
    update_energy = total([spread[k] * root_wide[k] for k in range(experts)]) / experts
    grad_energy = total([unit[k] * gram_mean[k] for k in range(experts)]) / experts
    graft = jnp.sqrt((grad_energy + energy_floor) / (update_energy + energy_floor))[:1]
    for start in range(0, width, LANES):
        columns = slice(start, start + LANES)
        products = mine[0] * held[0, :, columns].astype(jnp.float32)
        for g in range(1, experts):
            products = products + mine[g] * held[g, :, columns].astype(jnp.float32)
        mixed = products.astype(jnp.bfloat16)
        update_ref[0, :, columns] = (graft * mixed.astype(jnp.float32)).astype(jnp.bfloat16)


def gathered_body(gradient, prior_stat):
    owners = lax.axis_size("expert")
    experts = prior_stat.shape[0]
    slab_rows, width = gradient.shape[1:]
    keep = pltpu.VMEM((experts, experts, LANES), jnp.float32)
    return pl.pallas_call(
        functools.partial(kernel, owners),
        out_shape=(
            jax.ShapeDtypeStruct(gradient.shape, jnp.bfloat16),
            jax.ShapeDtypeStruct(prior_stat.shape, jnp.float32),
        ),
        in_specs=[pl.BlockSpec(memory_space=pl.ANY), pl.BlockSpec(memory_space=pltpu.VMEM)],
        out_specs=(pl.BlockSpec(memory_space=pltpu.VMEM), pl.BlockSpec(memory_space=pltpu.VMEM)),
        scratch_shapes=[
            pltpu.VMEM((experts, slab_rows, width), jnp.bfloat16),
            keep,
            keep,
            keep,
            keep,
            pltpu.SemaphoreType.DMA,
            pltpu.SemaphoreType.DMA((owners,)),
            pltpu.SemaphoreType.DMA((owners,)),
        ],
        compiler_params=pltpu.CompilerParams(collective_id=0, has_side_effects=True),
        name="shampoo_step",
    )(gradient, prior_stat)


def body(gradient, prior_stat):
    owners = lax.axis_size("expert")
    experts = prior_stat.shape[0]
    gathered_bytes = 2 * experts * gradient.shape[1] * gradient.shape[2]
    fits = gathered_bytes <= VMEM_BUDGET and experts == owners and experts == 8
    regular = gradient.shape[1] % 16 == 0 and gradient.shape[2] % LANES == 0
    if fits and regular:
        return gathered_body(gradient, prior_stat)
    return wide_body(gradient, prior_stat)


def solution(mesh):
    placed = (P(("layer", "expert"), None, None), P("layer", None))
    return jax.shard_map(
        body,
        mesh=mesh,
        in_specs=placed,
        out_specs=(P(("layer", "expert"), None, None), P("layer", None)),
        check_vma=False,
    )
```

```python
import functools

import jax
import jax.numpy as jnp
from jax import lax
from jax.experimental import pallas as pl
from jax.experimental.pallas import tpu as pltpu
from jax.sharding import PartitionSpec as P

ITERS = 5
ridge_rate = 0.001
energy_floor = 1e-06
LANES = 128
VMEM_BUDGET = 16 * 1024 * 1024
KERNEL_VMEM = 32 * 1024 * 1024
PAIR = 2
RING = 4
COPIES = 13


def matmul_high(left, right):
    return jnp.dot(left, right, precision=lax.Precision.HIGHEST, preferred_element_type=jnp.float32)


def inverse_root(statistic):
    count_rows = statistic.shape[0]
    identity = jnp.eye(count_rows, dtype=jnp.float32)
    ridge_term = ridge_rate * jnp.trace(statistic) / count_rows
    shifted = statistic + ridge_term * identity
    start_scale = 2.5 / jnp.sqrt(jnp.sum(shifted * shifted))
    matrix = start_scale * shifted
    root = start_scale**0.25 * identity
    for repeat in range(ITERS):
        factor = 1.25 * identity - 0.25 * matrix
        root = matmul_high(root, factor)
        square = matmul_high(factor, factor)
        matrix = matmul_high(matmul_high(square, square), matrix)
    return root


def apply_graft(mixed_bf, graft):
    fenced = lax.optimization_barrier(mixed_bf)
    return (graft * fenced.astype(jnp.float32)).astype(jnp.bfloat16)


def slice_grams(pieces):
    grams = jnp.einsum("eqrf,gqrf->eqrg", pieces, pieces, preferred_element_type=jnp.float32)
    return (pieces, grams)


def wide_body(gradient, prior_stat):
    experts = prior_stat.shape[0]
    owners = lax.axis_size("expert")
    local_experts = gradient.shape[0]
    slab_rows = gradient.shape[1]
    width = gradient.shape[2]
    entry_count = slab_rows * width
    slice_rows = slab_rows // owners
    blocked = gradient.reshape(local_experts, owners, slice_rows, width)
    regrouped, row_grams = slice_grams(
        lax.all_to_all(blocked, "expert", split_axis=1, concat_axis=0, tiled=True)
    )
    summed = lax.psum(jnp.sum(row_grams, axis=(1, 2)), "expert")
    gram_mean = summed / entry_count
    statistic = prior_stat + gram_mean
    root_bf = inverse_root(statistic).astype(jnp.bfloat16)
    flattened = regrouped.reshape(experts, -1)
    products = jnp.dot(root_bf, flattened, preferred_element_type=jnp.float32)
    mixed_bf = products.astype(jnp.bfloat16).reshape(experts, slice_rows, width)
    root_wide = root_bf.astype(jnp.float32)
    update_energy = jnp.sum(matmul_high(root_wide, gram_mean) * root_wide) / experts
    grad_energy = jnp.trace(gram_mean) / experts
    graft = jnp.sqrt((grad_energy + energy_floor) / (update_energy + energy_floor))
    grafted = apply_graft(mixed_bf, graft)
    update = lax.all_to_all(grafted, "expert", split_axis=0, concat_axis=1, tiled=True)
    return (update, statistic)


def splat_rows(columns, keep):
    for m, column in enumerate(columns):
        keep[m] = column


def entry(keep, k, m):
    return jnp.broadcast_to(keep[m, k : k + 1, :], keep.shape[1:])


def times(left, keep):
    size = len(left)
    out = []
    for m in range(size):
        terms = [left[k] * entry(keep, k, m) for k in range(size)]
        while len(terms) > 1:
            terms = [terms[i] + terms[i + 1] if i + 1 < len(terms) else terms[i] for i in range(0, len(terms), 2)]
        out.append(terms[0])
    return out


def total(tiles):
    acc = tiles[0]
    for tile in tiles[1:]:
        acc = acc + tile
    return jnp.broadcast_to(jnp.sum(acc, axis=0, keepdims=True), acc.shape)


def kernel(
    owners, gradient_ref, prior_hbm, mixed_ref, statistic_ref, graft_ref, held, keep_gram, keep_matrix, keep_factor,
    keep_square, prior_ref, local_sem, prior_sem, send_sem, recv_sem,
):
    me = lax.axis_index("expert")
    experts = owners
    slab_rows, width = held.shape[1:]
    rows = experts * slab_rows
    half = slab_rows // 2
    ring = owners // PAIR
    place, side = me // PAIR, me % PAIR

    def at(step, flip):
        return lax.rem(place + step + ring, ring) * PAIR + lax.rem(side + flip, PAIR)

    peers = [(0, 1), (1, 0), (-1, 0), (1, 1), (-1, 1)]
    barrier = pltpu.get_barrier_semaphore()
    for step, flip in peers:
        pl.semaphore_signal(
            barrier, inc=1, device_id={"expert": at(step, flip)}, device_id_type=pl.DeviceIdType.MESH
        )
    local = pltpu.make_async_copy(gradient_ref.at[0], held.at[me], local_sem)
    local.start()
    prior_copy = pltpu.make_async_copy(prior_hbm, prior_ref, prior_sem)
    prior_copy.start()
    pl.semaphore_wait(barrier, len(peers))

    made = []

    def send(source, owner, part, step, flip):
        span = slice(None) if part is None else pl.ds(part * half, half)
        copy = pltpu.make_async_remote_copy(
            src_ref=source.at[span],
            dst_ref=held.at[owner, span],
            send_sem=send_sem.at[len(made)],
            recv_sem=recv_sem.at[len(made)],
            device_id={"expert": at(step, flip)},
            device_id_type=pl.DeviceIdType.MESH,
        )
        copy.start()
        made.append(copy)
        return copy

    own = gradient_ref.at[0]
    first = [send(own, me, 0 if step > 0 else 1, step, flip) for flip in (0, 1) for step in (1, -1)]
    rest = [send(own, me, None, 0, 1)]
    rest += [send(own, me, 1 if step > 0 else 0, step, flip) for flip in (0, 1) for step in (1, -1)]
    index = 0
    for flip in (0, 1):
        for step in (1, -1):
            first[index].wait_recv()
            owner = at(-step, flip)
            rest.append(send(held.at[owner], owner, 0 if step > 0 else 1, step, 0))
            index += 1

    tile = (experts, LANES)
    row = lax.broadcasted_iota(jnp.int32, tile, 0)
    lane = lax.broadcasted_iota(jnp.int32, tile, 1)
    unit = [jnp.where(row == k, 1.0, 0.0).astype(jnp.float32) for k in range(experts)]
    prior_copy.wait()
    prior_wide = [jnp.broadcast_to(prior_ref[:, k : k + 1], tile) for k in range(experts)]

    local.wait()
    for copy in rest:
        copy.wait_recv()
    for copy in made:
        copy.wait_send()

    flat = held[...].reshape(rows, width)
    full = lax.dot_general(flat, flat, (((1,), (1,)), ((), ())), preferred_element_type=jnp.float32)
    own = lax.broadcasted_iota(jnp.int32, (rows, rows), 0) % slab_rows
    other = lax.broadcasted_iota(jnp.int32, (rows, rows), 1) % slab_rows
    diagonal = jnp.where(own == other, full, 0.0)
    paired = jnp.sum(diagonal.reshape(experts, slab_rows, rows), axis=1)
    column_of = lax.broadcasted_iota(jnp.int32, (experts, rows), 1) // slab_rows
    gram_mean = [
        jnp.broadcast_to(
            jnp.sum(jnp.where(column_of == k, paired, 0.0), axis=1, keepdims=True) / (slab_rows * width), tile
        )
        for k in range(experts)
    ]
    splat_rows(gram_mean, keep_gram)
    statistic = [prior_wide[k] + gram_mean[k] for k in range(experts)]
    shown = statistic[0]
    for k in range(1, experts):
        shown = jnp.where(lane == k, statistic[k], shown)
    statistic_ref[...] = shown

    ridge_term = ridge_rate * total([unit[k] * statistic[k] for k in range(experts)]) / experts
    shifted = [statistic[k] + ridge_term * unit[k] for k in range(experts)]
    start_scale = 2.5 / jnp.sqrt(total([s * s for s in shifted]))
    matrix = [start_scale * s for s in shifted]
    start_root = jnp.sqrt(jnp.sqrt(start_scale))
    root = [start_root * u for u in unit]
    for repeat in range(ITERS):
        factor = [1.25 * unit[k] - 0.25 * matrix[k] for k in range(experts)]
        splat_rows(factor, keep_factor)
        if repeat == 0:
            root = [start_root * f for f in factor]
        else:
            root = times(root, keep_factor)
        if repeat < ITERS - 1:
            splat_rows(matrix, keep_matrix)
            square = times(factor, keep_factor)
            splat_rows(square, keep_square)
            matrix = times(times(square, keep_square), keep_matrix)

    root_wide = [r.astype(jnp.bfloat16).astype(jnp.float32) for r in root]
    splat_rows(root_wide, keep_factor)
    mine = [jnp.broadcast_to(keep_factor[g, pl.ds(me, 1), :], tile)[:1] for g in range(experts)]
    spread = times(root_wide, keep_gram)
    update_energy = total([spread[k] * root_wide[k] for k in range(experts)]) / experts
    grad_energy = total([unit[k] * gram_mean[k] for k in range(experts)]) / experts
    graft = jnp.sqrt((grad_energy + energy_floor) / (update_energy + energy_floor))
    graft_ref[...] = graft
    for start in range(0, width, LANES):
        columns = slice(start, start + LANES)
        products = mine[0] * held[0, :, columns].astype(jnp.float32)
        for g in range(1, experts):
            products = products + mine[g] * held[g, :, columns].astype(jnp.float32)
        mixed_ref[:, columns] = products.astype(jnp.bfloat16)


def finish(mixed_ref, wide_ref, graft_ref, update_ref, statistic_ref):
    graft = graft_ref[:1]
    for start in range(0, mixed_ref.shape[1], LANES):
        columns = slice(start, start + LANES)
        mixed = mixed_ref[:, columns].astype(jnp.float32)
        update_ref[0, :, columns] = (graft * mixed).astype(jnp.bfloat16)
    statistic_ref[...] = wide_ref[:, : statistic_ref.shape[1]]


def gathered_body(gradient, prior_stat):
    owners = lax.axis_size("expert")
    experts = prior_stat.shape[0]
    slab_rows, width = gradient.shape[1:]
    keep = pltpu.VMEM((experts, experts, LANES), jnp.float32)
    vmem = pl.BlockSpec(memory_space=pltpu.VMEM)
    mixed, wide, graft = pl.pallas_call(
        functools.partial(kernel, owners),
        out_shape=(
            pltpu.VMEM((slab_rows, width), jnp.bfloat16),
            pltpu.VMEM((experts, LANES), jnp.float32),
            pltpu.VMEM((experts, LANES), jnp.float32),
        ),
        in_specs=[pl.BlockSpec(memory_space=pltpu.HBM)] * 2,
        out_specs=(vmem, vmem, vmem),
        scratch_shapes=[
            pltpu.VMEM((experts, slab_rows, width), jnp.bfloat16),
            keep,
            keep,
            keep,
            keep,
            pltpu.VMEM(prior_stat.shape, jnp.float32),
            pltpu.SemaphoreType.DMA,
            pltpu.SemaphoreType.DMA,
            pltpu.SemaphoreType.DMA((COPIES,)),
            pltpu.SemaphoreType.DMA((COPIES,)),
        ],
        compiler_params=pltpu.CompilerParams(
            collective_id=0, has_side_effects=True, vmem_limit_bytes=KERNEL_VMEM
        ),
        name="shampoo_step",
    )(gradient, prior_stat)
    return pl.pallas_call(
        finish,
        out_shape=(
            jax.ShapeDtypeStruct(gradient.shape, jnp.bfloat16),
            jax.ShapeDtypeStruct(prior_stat.shape, jnp.float32),
        ),
        in_specs=[vmem, vmem, vmem],
        out_specs=(vmem, vmem),
        compiler_params=pltpu.CompilerParams(vmem_limit_bytes=KERNEL_VMEM),
        name="finish",
    )(mixed, wide, graft)


def body(gradient, prior_stat):
    owners = lax.axis_size("expert")
    experts = prior_stat.shape[0]
    gathered_bytes = 2 * experts * gradient.shape[1] * gradient.shape[2]
    fits = gathered_bytes <= VMEM_BUDGET and experts == owners and owners == PAIR * RING
    regular = gradient.shape[1] % 16 == 0 and gradient.shape[2] % LANES == 0
    if fits and regular:
        return gathered_body(gradient, prior_stat)
    return wide_body(gradient, prior_stat)


def solution(mesh):
    placed = (P(("layer", "expert"), None, None), P("layer", None))
    return jax.shard_map(
        body,
        mesh=mesh,
        in_specs=placed,
        out_specs=(P(("layer", "expert"), None, None), P("layer", None)),
        check_vma=False,
    )
```

```python
import functools

import jax
import jax.numpy as jnp
from jax import lax
from jax.experimental import pallas as pl
from jax.experimental.pallas import tpu as pltpu
from jax.sharding import PartitionSpec as P

ITERS = 5
ridge_rate = 0.001
energy_floor = 1e-06
LANES = 128
VMEM_BUDGET = 16 * 1024 * 1024
KERNEL_VMEM = 32 * 1024 * 1024
PAIR = 2


def matmul_high(left, right):
    return jnp.dot(left, right, precision=lax.Precision.HIGHEST, preferred_element_type=jnp.float32)


def inverse_root(statistic):
    count_rows = statistic.shape[0]
    identity = jnp.eye(count_rows, dtype=jnp.float32)
    ridge_term = ridge_rate * jnp.trace(statistic) / count_rows
    shifted = statistic + ridge_term * identity
    start_scale = 2.5 / jnp.sqrt(jnp.sum(shifted * shifted))
    matrix = start_scale * shifted
    root = start_scale**0.25 * identity
    for repeat in range(ITERS):
        factor = 1.25 * identity - 0.25 * matrix
        root = matmul_high(root, factor)
        square = matmul_high(factor, factor)
        matrix = matmul_high(matmul_high(square, square), matrix)
    return root


def apply_graft(mixed_bf, graft):
    fenced = lax.optimization_barrier(mixed_bf)
    return (graft * fenced.astype(jnp.float32)).astype(jnp.bfloat16)


def slice_grams(pieces):
    grams = jnp.einsum("eqrf,gqrf->eqrg", pieces, pieces, preferred_element_type=jnp.float32)
    return (pieces, grams)


def wide_body(gradient, prior_stat):
    experts = prior_stat.shape[0]
    owners = lax.axis_size("expert")
    local_experts = gradient.shape[0]
    slab_rows = gradient.shape[1]
    width = gradient.shape[2]
    entry_count = slab_rows * width
    slice_rows = slab_rows // owners
    blocked = gradient.reshape(local_experts, owners, slice_rows, width)
    regrouped, row_grams = slice_grams(
        lax.all_to_all(blocked, "expert", split_axis=1, concat_axis=0, tiled=True)
    )
    summed = lax.psum(jnp.sum(row_grams, axis=(1, 2)), "expert")
    gram_mean = summed / entry_count
    statistic = prior_stat + gram_mean
    root_bf = inverse_root(statistic).astype(jnp.bfloat16)
    flattened = regrouped.reshape(experts, -1)
    products = jnp.dot(root_bf, flattened, preferred_element_type=jnp.float32)
    mixed_bf = products.astype(jnp.bfloat16).reshape(experts, slice_rows, width)
    root_wide = root_bf.astype(jnp.float32)
    update_energy = jnp.sum(matmul_high(root_wide, gram_mean) * root_wide) / experts
    grad_energy = jnp.trace(gram_mean) / experts
    graft = jnp.sqrt((grad_energy + energy_floor) / (update_energy + energy_floor))
    grafted = apply_graft(mixed_bf, graft)
    update = lax.all_to_all(grafted, "expert", split_axis=0, concat_axis=1, tiled=True)
    return (update, statistic)


def splat_rows(columns, keep):
    for m, column in enumerate(columns):
        keep[m] = column


def entry(keep, k, m):
    return jnp.broadcast_to(keep[m, k : k + 1, :], keep.shape[1:])


def times(left, keep):
    size = len(left)
    out = []
    for m in range(size):
        terms = [left[k] * entry(keep, k, m) for k in range(size)]
        while len(terms) > 1:
            terms = [terms[i] + terms[i + 1] if i + 1 < len(terms) else terms[i] for i in range(0, len(terms), 2)]
        out.append(terms[0])
    return out


def total(tiles):
    acc = tiles[0]
    for tile in tiles[1:]:
        acc = acc + tile
    return jnp.broadcast_to(jnp.sum(acc, axis=0, keepdims=True), acc.shape)


def kernel(
    owners, gradient_ref, prior_hbm, mixed_ref, statistic_ref, graft_ref, held, keep_gram, keep_matrix, keep_factor,
    keep_square, prior_ref, local_sem, prior_sem, send_sem, recv_sem, up_ready, cross_ready,
):
    me = lax.axis_index("expert")
    experts = owners
    slab_rows, width = held.shape[1:]
    rows = experts * slab_rows
    line = owners // PAIR
    last = line - 1
    place, side = me // PAIR, me % PAIR
    partner = place * PAIR + 1 - side
    opposite = (last - place) * PAIR + 1 - side

    def here(position):
        return position * PAIR + side

    def signal(semaphore, device):
        pl.semaphore_signal(semaphore, inc=1, device_id={"expert": device}, device_id_type=pl.DeviceIdType.MESH)

    def copy(source, owner, sem, device):
        return pltpu.make_async_remote_copy(
            src_ref=source,
            dst_ref=held.at[owner],
            send_sem=send_sem.at[sem],
            recv_sem=recv_sem.at[owner],
            device_id={"expert": device},
            device_id_type=pl.DeviceIdType.MESH,
        )

    CROSS, UP, DOWN, FAR = 0, line, 2 * line, 3 * line
    own = gradient_ref.at[0]

    barrier = pltpu.get_barrier_semaphore()

    @pl.when(side == 0)
    def _():
        signal(barrier, partner)

    @pl.when(place == 0)
    def _():
        signal(barrier, opposite)

    for position in range(1, line):

        @pl.when(position > place)
        def _():
            signal(barrier, here(position))

    local = pltpu.make_async_copy(own, held.at[me], local_sem)
    local.start()
    prior_copy = pltpu.make_async_copy(prior_hbm, prior_ref, prior_sem)
    prior_copy.start()
    greeted = place + side + place // last

    @pl.when(greeted > 0)
    def _():
        pl.semaphore_wait(barrier, greeted)

    @pl.when(place == last)
    def _():
        copy(own, me, FAR, opposite).start()

    for position in range(last):

        @pl.when(position < place)
        def _():
            copy(own, me, DOWN + position, here(position)).start()

    @pl.when(place > 0)
    def _():
        signal(up_ready, here(place - 1))

    @pl.when(side == 1)
    def _():
        signal(cross_ready, partner)

    @pl.when(side == 0)
    def _():
        pl.semaphore_wait(cross_ready, 1)

    copy(own, me, CROSS + place, partner).start()

    @pl.when(place < last)
    def _():
        pl.semaphore_wait(up_ready, 1)
        copy(own, me, UP + place, here(place + 1)).start()

    for distance in range(1, line):

        @pl.when(place + distance <= last)
        def _():
            position = place + distance
            block = here(position)
            copy(own, block, CROSS, partner).wait_recv()

            if distance < last:
                copy(held.at[block], block, CROSS + position, partner).start()

        @pl.when(place - distance >= 0)
        def _():
            position = place - distance
            block = here(position)
            copy(own, block, CROSS, partner).wait_recv()
            copy(held.at[block], block, CROSS + position, partner).start()

            @pl.when(place < last)
            def _():
                copy(held.at[block], block, UP + position, here(place + 1)).start()

    tile = (experts, LANES)
    row = lax.broadcasted_iota(jnp.int32, tile, 0)
    lane = lax.broadcasted_iota(jnp.int32, tile, 1)
    unit = [jnp.where(row == k, 1.0, 0.0).astype(jnp.float32) for k in range(experts)]
    prior_copy.wait()
    prior_wide = [jnp.broadcast_to(prior_ref[:, k : k + 1], tile) for k in range(experts)]

    local.wait()
    for position in range(line):
        copy(own, position * PAIR + 1 - side, CROSS, partner).wait_recv()

    flat = held[...].reshape(rows, width)
    full = lax.dot_general(flat, flat, (((1,), (1,)), ((), ())), preferred_element_type=jnp.float32)
    left_row = lax.broadcasted_iota(jnp.int32, (rows, rows), 0) % slab_rows
    right_row = lax.broadcasted_iota(jnp.int32, (rows, rows), 1) % slab_rows
    diagonal = jnp.where(left_row == right_row, full, 0.0)
    paired = jnp.sum(diagonal.reshape(experts, slab_rows, rows), axis=1)
    column_of = lax.broadcasted_iota(jnp.int32, (experts, rows), 1) // slab_rows
    gram_mean = [
        jnp.broadcast_to(
            jnp.sum(jnp.where(column_of == k, paired, 0.0), axis=1, keepdims=True) / (slab_rows * width), tile
        )
        for k in range(experts)
    ]
    splat_rows(gram_mean, keep_gram)
    statistic = [prior_wide[k] + gram_mean[k] for k in range(experts)]
    shown = statistic[0]
    for k in range(1, experts):
        shown = jnp.where(lane == k, statistic[k], shown)
    statistic_ref[...] = shown

    ridge_term = ridge_rate * total([unit[k] * statistic[k] for k in range(experts)]) / experts
    shifted = [statistic[k] + ridge_term * unit[k] for k in range(experts)]
    start_scale = 2.5 / jnp.sqrt(total([s * s for s in shifted]))
    matrix = [start_scale * s for s in shifted]
    start_root = jnp.sqrt(jnp.sqrt(start_scale))
    root = [start_root * u for u in unit]
    for repeat in range(ITERS):
        factor = [1.25 * unit[k] - 0.25 * matrix[k] for k in range(experts)]
        splat_rows(factor, keep_factor)
        if repeat == 0:
            root = [start_root * f for f in factor]
        else:
            root = times(root, keep_factor)
        if repeat < ITERS - 1:
            splat_rows(matrix, keep_matrix)
            square = times(factor, keep_factor)
            splat_rows(square, keep_square)
            matrix = times(times(square, keep_square), keep_matrix)

    root_wide = [r.astype(jnp.bfloat16).astype(jnp.float32) for r in root]
    splat_rows(root_wide, keep_factor)
    mine = [jnp.broadcast_to(keep_factor[g, pl.ds(me, 1), :], tile)[:1] for g in range(experts)]
    spread = times(root_wide, keep_gram)
    update_energy = total([spread[k] * root_wide[k] for k in range(experts)]) / experts
    grad_energy = total([unit[k] * gram_mean[k] for k in range(experts)]) / experts
    graft = jnp.sqrt((grad_energy + energy_floor) / (update_energy + energy_floor))
    graft_ref[...] = graft
    for start in range(0, width, LANES):
        columns = slice(start, start + LANES)
        products = mine[0] * held[0, :, columns].astype(jnp.float32)
        for g in range(1, experts):
            products = products + mine[g] * held[g, :, columns].astype(jnp.float32)
        mixed_ref[:, columns] = products.astype(jnp.bfloat16)

    for position in range(line):

        @pl.when((place > 0) | (position < last))
        def _():
            copy(own, me, CROSS + position, partner).wait_send()

        @pl.when((position <= place) & (place < last))
        def _():
            copy(own, me, UP + position, partner).wait_send()

        @pl.when(position < place)
        def _():
            copy(own, me, DOWN + position, partner).wait_send()

    @pl.when(place == last)
    def _():
        copy(own, me, FAR, partner).wait_send()


def finish(mixed_ref, wide_ref, graft_ref, update_ref, statistic_ref):
    graft = graft_ref[:1]
    for start in range(0, mixed_ref.shape[1], LANES):
        columns = slice(start, start + LANES)
        mixed = mixed_ref[:, columns].astype(jnp.float32)
        update_ref[0, :, columns] = (graft * mixed).astype(jnp.bfloat16)
    statistic_ref[...] = wide_ref[:, : statistic_ref.shape[1]]


def gathered_body(gradient, prior_stat):
    owners = lax.axis_size("expert")
    experts = prior_stat.shape[0]
    slab_rows, width = gradient.shape[1:]
    keep = pltpu.VMEM((experts, experts, LANES), jnp.float32)
    vmem = pl.BlockSpec(memory_space=pltpu.VMEM)
    mixed, wide, graft = pl.pallas_call(
        functools.partial(kernel, owners),
        out_shape=(
            pltpu.VMEM((slab_rows, width), jnp.bfloat16),
            pltpu.VMEM((experts, LANES), jnp.float32),
            pltpu.VMEM((experts, LANES), jnp.float32),
        ),
        in_specs=[pl.BlockSpec(memory_space=pltpu.HBM)] * 2,
        out_specs=(vmem, vmem, vmem),
        scratch_shapes=[
            pltpu.VMEM((experts, slab_rows, width), jnp.bfloat16),
            keep,
            keep,
            keep,
            keep,
            pltpu.VMEM(prior_stat.shape, jnp.float32),
            pltpu.SemaphoreType.DMA,
            pltpu.SemaphoreType.DMA,
            pltpu.SemaphoreType.DMA((3 * owners // PAIR + 1,)),
            pltpu.SemaphoreType.DMA((owners,)),
            pltpu.SemaphoreType.REGULAR,
            pltpu.SemaphoreType.REGULAR,
        ],
        compiler_params=pltpu.CompilerParams(
            collective_id=0, has_side_effects=True, vmem_limit_bytes=KERNEL_VMEM
        ),
        name="shampoo_step",
    )(*[pltpu.with_memory_space_constraint(x, pltpu.HBM) for x in (gradient, prior_stat)])
    return pl.pallas_call(
        finish,
        out_shape=(
            jax.ShapeDtypeStruct(gradient.shape, jnp.bfloat16),
            jax.ShapeDtypeStruct(prior_stat.shape, jnp.float32),
        ),
        in_specs=[vmem, vmem, vmem],
        out_specs=(vmem, vmem),
        compiler_params=pltpu.CompilerParams(vmem_limit_bytes=KERNEL_VMEM),
        name="finish",
    )(mixed, wide, graft)


def body(gradient, prior_stat):
    owners = lax.axis_size("expert")
    experts = prior_stat.shape[0]
    gathered_bytes = 2 * experts * gradient.shape[1] * gradient.shape[2]
    fits = gathered_bytes <= VMEM_BUDGET and experts == owners and owners % PAIR == 0 and 2 * PAIR <= owners <= 8
    regular = gradient.shape[1] % 16 == 0 and gradient.shape[2] % LANES == 0
    if fits and regular:
        return gathered_body(gradient, prior_stat)
    return wide_body(gradient, prior_stat)


def solution(mesh):
    placed = (P(("layer", "expert"), None, None), P("layer", None))
    return jax.shard_map(
        body,
        mesh=mesh,
        in_specs=placed,
        out_specs=(P(("layer", "expert"), None, None), P("layer", None)),
        check_vma=False,
    )
```

```python
import functools

import jax
import jax.numpy as jnp
from jax import lax
from jax.experimental import pallas as pl
from jax.experimental.pallas import tpu as pltpu
from jax.sharding import PartitionSpec as P

ITERS = 5
ridge_rate = 0.001
energy_floor = 1e-06
LANES = 128
VMEM_BUDGET = 16 * 1024 * 1024
KERNEL_VMEM = 32 * 1024 * 1024
PAIR = 2
RING = 4
COPIES = 13


def matmul_high(left, right):
    return jnp.dot(left, right, precision=lax.Precision.HIGHEST, preferred_element_type=jnp.float32)


def inverse_root(statistic):
    count_rows = statistic.shape[0]
    identity = jnp.eye(count_rows, dtype=jnp.float32)
    ridge_term = ridge_rate * jnp.trace(statistic) / count_rows
    shifted = statistic + ridge_term * identity
    start_scale = 2.5 / jnp.sqrt(jnp.sum(shifted * shifted))
    matrix = start_scale * shifted
    root = start_scale**0.25 * identity
    for repeat in range(ITERS):
        factor = 1.25 * identity - 0.25 * matrix
        root = matmul_high(root, factor)
        square = matmul_high(factor, factor)
        matrix = matmul_high(matmul_high(square, square), matrix)
    return root


def apply_graft(mixed_bf, graft):
    fenced = lax.optimization_barrier(mixed_bf)
    return (graft * fenced.astype(jnp.float32)).astype(jnp.bfloat16)


def slice_grams(pieces):
    grams = jnp.einsum("eqrf,gqrf->eqrg", pieces, pieces, preferred_element_type=jnp.float32)
    return (pieces, grams)


def wide_body(gradient, prior_stat):
    experts = prior_stat.shape[0]
    owners = lax.axis_size("expert")
    local_experts = gradient.shape[0]
    slab_rows = gradient.shape[1]
    width = gradient.shape[2]
    entry_count = slab_rows * width
    slice_rows = slab_rows // owners
    blocked = gradient.reshape(local_experts, owners, slice_rows, width)
    regrouped, row_grams = slice_grams(
        lax.all_to_all(blocked, "expert", split_axis=1, concat_axis=0, tiled=True)
    )
    summed = lax.psum(jnp.sum(row_grams, axis=(1, 2)), "expert")
    gram_mean = summed / entry_count
    statistic = prior_stat + gram_mean
    root_bf = inverse_root(statistic).astype(jnp.bfloat16)
    flattened = regrouped.reshape(experts, -1)
    products = jnp.dot(root_bf, flattened, preferred_element_type=jnp.float32)
    mixed_bf = products.astype(jnp.bfloat16).reshape(experts, slice_rows, width)
    root_wide = root_bf.astype(jnp.float32)
    update_energy = jnp.sum(matmul_high(root_wide, gram_mean) * root_wide) / experts
    grad_energy = jnp.trace(gram_mean) / experts
    graft = jnp.sqrt((grad_energy + energy_floor) / (update_energy + energy_floor))
    grafted = apply_graft(mixed_bf, graft)
    update = lax.all_to_all(grafted, "expert", split_axis=0, concat_axis=1, tiled=True)
    return (update, statistic)


def splat_rows(columns, keep):
    for m, column in enumerate(columns):
        keep[m] = column


def entry(keep, k, m):
    return jnp.broadcast_to(keep[m, k : k + 1, :], keep.shape[1:])


def times(left, keep):
    size = len(left)
    out = []
    for m in range(size):
        terms = [left[k] * entry(keep, k, m) for k in range(size)]
        while len(terms) > 1:
            terms = [terms[i] + terms[i + 1] if i + 1 < len(terms) else terms[i] for i in range(0, len(terms), 2)]
        out.append(terms[0])
    return out


def total(tiles):
    acc = tiles[0]
    for tile in tiles[1:]:
        acc = acc + tile
    return jnp.broadcast_to(jnp.sum(acc, axis=0, keepdims=True), acc.shape)


def kernel(
    owners, gradient_ref, prior_hbm, mixed_ref, statistic_ref, graft_ref, held, keep_gram, keep_matrix, keep_factor,
    keep_square, prior_ref, local_sem, prior_sem, send_sem, recv_sem,
):
    me = lax.axis_index("expert")
    experts = owners
    slab_rows, width = held.shape[1:]
    rows = experts * slab_rows
    half = slab_rows // 2
    ring = owners // PAIR
    place, side = me // PAIR, me % PAIR

    def at(step, flip):
        return lax.rem(place + step + ring, ring) * PAIR + lax.rem(side + flip, PAIR)

    peers = [(0, 1), (1, 0), (-1, 0), (1, 1), (-1, 1)]
    barrier = pltpu.get_barrier_semaphore()
    for step, flip in peers:
        pl.semaphore_signal(
            barrier, inc=1, device_id={"expert": at(step, flip)}, device_id_type=pl.DeviceIdType.MESH
        )
    local = pltpu.make_async_copy(gradient_ref.at[0], held.at[me], local_sem)
    local.start()
    prior_copy = pltpu.make_async_copy(prior_hbm, prior_ref, prior_sem)
    prior_copy.start()
    pl.semaphore_wait(barrier, len(peers))

    made = []

    def send(source, owner, part, step, flip):
        span = slice(None) if part is None else pl.ds(part * half, half)
        copy = pltpu.make_async_remote_copy(
            src_ref=source.at[span],
            dst_ref=held.at[owner, span],
            send_sem=send_sem.at[len(made)],
            recv_sem=recv_sem.at[len(made)],
            device_id={"expert": at(step, flip)},
            device_id_type=pl.DeviceIdType.MESH,
        )
        copy.start()
        made.append(copy)
        return copy

    own = gradient_ref.at[0]
    first = [send(own, me, 0 if step > 0 else 1, step, flip) for flip in (0, 1) for step in (1, -1)]
    rest = [send(own, me, None, 0, 1)]
    rest += [send(own, me, 1 if step > 0 else 0, step, flip) for flip in (0, 1) for step in (1, -1)]
    index = 0
    for flip in (0, 1):
        for step in (1, -1):
            first[index].wait_recv()
            owner = at(-step, flip)
            rest.append(send(held.at[owner], owner, 0 if step > 0 else 1, step, 0))
            index += 1

    tile = (experts, LANES)
    row = lax.broadcasted_iota(jnp.int32, tile, 0)
    lane = lax.broadcasted_iota(jnp.int32, tile, 1)
    unit = [jnp.where(row == k, 1.0, 0.0).astype(jnp.float32) for k in range(experts)]
    prior_copy.wait()
    prior_wide = [jnp.broadcast_to(prior_ref[:, k : k + 1], tile) for k in range(experts)]

    local.wait()
    for copy in rest:
        copy.wait_recv()
    for copy in made:
        copy.wait_send()

    flat = held[...].reshape(rows, width)
    full = lax.dot_general(flat, flat, (((1,), (1,)), ((), ())), preferred_element_type=jnp.float32)
    own = lax.broadcasted_iota(jnp.int32, (rows, rows), 0) % slab_rows
    other = lax.broadcasted_iota(jnp.int32, (rows, rows), 1) % slab_rows
    diagonal = jnp.where(own == other, full, 0.0)
    paired = jnp.sum(diagonal.reshape(experts, slab_rows, rows), axis=1)
    column_of = lax.broadcasted_iota(jnp.int32, (experts, rows), 1) // slab_rows
    gram_mean = [
        jnp.broadcast_to(
            jnp.sum(jnp.where(column_of == k, paired, 0.0), axis=1, keepdims=True) / (slab_rows * width), tile
        )
        for k in range(experts)
    ]
    splat_rows(gram_mean, keep_gram)
    statistic = [prior_wide[k] + gram_mean[k] for k in range(experts)]
    shown = statistic[0]
    for k in range(1, experts):
        shown = jnp.where(lane == k, statistic[k], shown)
    statistic_ref[...] = shown

    ridge_term = ridge_rate * total([unit[k] * statistic[k] for k in range(experts)]) / experts
    shifted = [statistic[k] + ridge_term * unit[k] for k in range(experts)]
    start_scale = 2.5 / jnp.sqrt(total([s * s for s in shifted]))
    matrix = [start_scale * s for s in shifted]
    start_root = jnp.sqrt(jnp.sqrt(start_scale))
    root = [start_root * u for u in unit]
    for repeat in range(ITERS):
        factor = [1.25 * unit[k] - 0.25 * matrix[k] for k in range(experts)]
        splat_rows(factor, keep_factor)
        if repeat == 0:
            root = [start_root * f for f in factor]
        else:
            root = times(root, keep_factor)
        if repeat < ITERS - 1:
            splat_rows(matrix, keep_matrix)
            square = times(factor, keep_factor)
            splat_rows(square, keep_square)
            matrix = times(times(square, keep_square), keep_matrix)

    root_wide = [r.astype(jnp.bfloat16).astype(jnp.float32) for r in root]
    splat_rows(root_wide, keep_factor)
    mine = [jnp.broadcast_to(keep_factor[g, pl.ds(me, 1), :], tile)[:1] for g in range(experts)]
    spread = times(root_wide, keep_gram)
    update_energy = total([spread[k] * root_wide[k] for k in range(experts)]) / experts
    grad_energy = total([unit[k] * gram_mean[k] for k in range(experts)]) / experts
    graft = jnp.sqrt((grad_energy + energy_floor) / (update_energy + energy_floor))
    graft_ref[...] = graft
    for start in range(0, width, LANES):
        columns = slice(start, start + LANES)
        products = mine[0] * held[0, :, columns].astype(jnp.float32)
        for g in range(1, experts):
            products = products + mine[g] * held[g, :, columns].astype(jnp.float32)
        mixed_ref[:, columns] = products.astype(jnp.bfloat16)


def finish(mixed_ref, wide_ref, graft_ref, update_ref, statistic_ref):
    graft = graft_ref[:1]
    for start in range(0, mixed_ref.shape[1], LANES):
        columns = slice(start, start + LANES)
        mixed = mixed_ref[:, columns].astype(jnp.float32)
        update_ref[0, :, columns] = (graft * mixed).astype(jnp.bfloat16)
    statistic_ref[...] = wide_ref[:, : statistic_ref.shape[1]]


def gathered_body(gradient, prior_stat):
    owners = lax.axis_size("expert")
    experts = prior_stat.shape[0]
    slab_rows, width = gradient.shape[1:]
    keep = pltpu.VMEM((experts, experts, LANES), jnp.float32)
    vmem = pl.BlockSpec(memory_space=pltpu.VMEM)
    mixed, wide, graft = pl.pallas_call(
        functools.partial(kernel, owners),
        out_shape=(
            pltpu.VMEM((slab_rows, width), jnp.bfloat16),
            pltpu.VMEM((experts, LANES), jnp.float32),
            pltpu.VMEM((experts, LANES), jnp.float32),
        ),
        in_specs=[pl.BlockSpec(memory_space=pltpu.HBM)] * 2,
        out_specs=(vmem, vmem, vmem),
        scratch_shapes=[
            pltpu.VMEM((experts, slab_rows, width), jnp.bfloat16),
            keep,
            keep,
            keep,
            keep,
            pltpu.VMEM(prior_stat.shape, jnp.float32),
            pltpu.SemaphoreType.DMA,
            pltpu.SemaphoreType.DMA,
            pltpu.SemaphoreType.DMA((COPIES,)),
            pltpu.SemaphoreType.DMA((COPIES,)),
        ],
        compiler_params=pltpu.CompilerParams(
            collective_id=0, has_side_effects=True, vmem_limit_bytes=KERNEL_VMEM
        ),
        name="shampoo_step",
    )(*[pltpu.with_memory_space_constraint(x, pltpu.HBM) for x in (gradient, prior_stat)])
    return pl.pallas_call(
        finish,
        out_shape=(
            jax.ShapeDtypeStruct(gradient.shape, jnp.bfloat16),
            jax.ShapeDtypeStruct(prior_stat.shape, jnp.float32),
        ),
        in_specs=[vmem, vmem, vmem],
        out_specs=(vmem, vmem),
        compiler_params=pltpu.CompilerParams(vmem_limit_bytes=KERNEL_VMEM),
        name="finish",
    )(mixed, wide, graft)


def body(gradient, prior_stat):
    owners = lax.axis_size("expert")
    experts = prior_stat.shape[0]
    gathered_bytes = 2 * experts * gradient.shape[1] * gradient.shape[2]
    fits = gathered_bytes <= VMEM_BUDGET and experts == owners and owners == PAIR * RING
    regular = gradient.shape[1] % 16 == 0 and gradient.shape[2] % LANES == 0
    if fits and regular:
        return gathered_body(gradient, prior_stat)
    return wide_body(gradient, prior_stat)


def solution(mesh):
    placed = (P(("layer", "expert"), None, None), P("layer", None))
    return jax.shard_map(
        body,
        mesh=mesh,
        in_specs=placed,
        out_specs=(P(("layer", "expert"), None, None), P("layer", None)),
        check_vma=False,
    )
```

```python
import functools

import jax
import jax.numpy as jnp
from jax import lax
from jax.experimental import pallas as pl
from jax.experimental.pallas import tpu as pltpu
from jax.sharding import PartitionSpec as P

ITERS = 5
ridge_rate = 0.001
energy_floor = 1e-06
LANES = 128
VMEM_BUDGET = 16 * 1024 * 1024
KERNEL_VMEM = 32 * 1024 * 1024


def matmul_high(left, right):
    return jnp.dot(left, right, precision=lax.Precision.HIGHEST, preferred_element_type=jnp.float32)


def inverse_root(statistic):
    count_rows = statistic.shape[0]
    identity = jnp.eye(count_rows, dtype=jnp.float32)
    ridge_term = ridge_rate * jnp.trace(statistic) / count_rows
    shifted = statistic + ridge_term * identity
    start_scale = 2.5 / jnp.sqrt(jnp.sum(shifted * shifted))
    matrix = start_scale * shifted
    root = start_scale**0.25 * identity
    for repeat in range(ITERS):
        factor = 1.25 * identity - 0.25 * matrix
        root = matmul_high(root, factor)
        square = matmul_high(factor, factor)
        matrix = matmul_high(matmul_high(square, square), matrix)
    return root


def apply_graft(mixed_bf, graft):
    fenced = lax.optimization_barrier(mixed_bf)
    return (graft * fenced.astype(jnp.float32)).astype(jnp.bfloat16)


def slice_grams(pieces):
    grams = jnp.einsum("eqrf,gqrf->eqrg", pieces, pieces, preferred_element_type=jnp.float32)
    return (pieces, grams)


def wide_body(gradient, prior_stat):
    experts = prior_stat.shape[0]
    owners = lax.axis_size("expert")
    local_experts = gradient.shape[0]
    slab_rows = gradient.shape[1]
    width = gradient.shape[2]
    entry_count = slab_rows * width
    slice_rows = slab_rows // owners
    blocked = gradient.reshape(local_experts, owners, slice_rows, width)
    regrouped, row_grams = slice_grams(
        lax.all_to_all(blocked, "expert", split_axis=1, concat_axis=0, tiled=True)
    )
    summed = lax.psum(jnp.sum(row_grams, axis=(1, 2)), "expert")
    gram_mean = summed / entry_count
    statistic = prior_stat + gram_mean
    root_bf = inverse_root(statistic).astype(jnp.bfloat16)
    flattened = regrouped.reshape(experts, -1)
    products = jnp.dot(root_bf, flattened, preferred_element_type=jnp.float32)
    mixed_bf = products.astype(jnp.bfloat16).reshape(experts, slice_rows, width)
    root_wide = root_bf.astype(jnp.float32)
    update_energy = jnp.sum(matmul_high(root_wide, gram_mean) * root_wide) / experts
    grad_energy = jnp.trace(gram_mean) / experts
    graft = jnp.sqrt((grad_energy + energy_floor) / (update_energy + energy_floor))
    grafted = apply_graft(mixed_bf, graft)
    update = lax.all_to_all(grafted, "expert", split_axis=0, concat_axis=1, tiled=True)
    return (update, statistic)


def splat_rows(columns, keep):
    for m, column in enumerate(columns):
        keep[m] = column


def entry(keep, k, m):
    return jnp.broadcast_to(keep[m, k : k + 1, :], keep.shape[1:])


def times(left, keep):
    size = len(left)
    out = []
    for m in range(size):
        terms = [left[k] * entry(keep, k, m) for k in range(size)]
        while len(terms) > 1:
            terms = [terms[i] + terms[i + 1] if i + 1 < len(terms) else terms[i] for i in range(0, len(terms), 2)]
        out.append(terms[0])
    return out


def total(tiles):
    acc = tiles[0]
    for tile in tiles[1:]:
        acc = acc + tile
    return jnp.broadcast_to(jnp.sum(acc, axis=0, keepdims=True), acc.shape)


def kernel(
    owners, gradient_ref, prior_hbm, mixed_ref, statistic_ref, graft_ref, held, keep_gram, keep_matrix, keep_factor,
    keep_square, prior_ref, local_sem, prior_sem, send_sem, recv_sem,
):
    me = lax.axis_index("expert")
    experts = owners
    slab_rows, width = held.shape[1:]
    rows = experts * slab_rows
    barrier = pltpu.get_barrier_semaphore()
    for step in range(1, owners):
        pl.semaphore_signal(
            barrier, inc=1, device_id={"expert": lax.rem(me + step, owners)}, device_id_type=pl.DeviceIdType.MESH
        )
    local = pltpu.make_async_copy(gradient_ref.at[0], held.at[me], local_sem)
    local.start()
    prior_copy = pltpu.make_async_copy(prior_hbm, prior_ref, prior_sem)
    prior_copy.start()
    pl.semaphore_wait(barrier, owners - 1)
    made = []
    for step in range(1, owners):
        copy = pltpu.make_async_remote_copy(
            src_ref=gradient_ref.at[0],
            dst_ref=held.at[me],
            send_sem=send_sem.at[step],
            recv_sem=recv_sem.at[step],
            device_id={"expert": lax.rem(me + step, owners)},
            device_id_type=pl.DeviceIdType.MESH,
        )
        copy.start()
        made.append(copy)

    tile = (experts, LANES)
    row = lax.broadcasted_iota(jnp.int32, tile, 0)
    lane = lax.broadcasted_iota(jnp.int32, tile, 1)
    unit = [jnp.where(row == k, 1.0, 0.0).astype(jnp.float32) for k in range(experts)]
    prior_copy.wait()
    prior_wide = [jnp.broadcast_to(prior_ref[:, k : k + 1], tile) for k in range(experts)]

    local.wait()
    for copy in made:
        copy.wait()

    flat = held[...].reshape(rows, width)
    full = lax.dot_general(flat, flat, (((1,), (1,)), ((), ())), preferred_element_type=jnp.float32)
    own = lax.broadcasted_iota(jnp.int32, (rows, rows), 0) % slab_rows
    other = lax.broadcasted_iota(jnp.int32, (rows, rows), 1) % slab_rows
    diagonal = jnp.where(own == other, full, 0.0)
    paired = jnp.sum(diagonal.reshape(experts, slab_rows, rows), axis=1)
    column_of = lax.broadcasted_iota(jnp.int32, (experts, rows), 1) // slab_rows
    gram_mean = [
        jnp.broadcast_to(
            jnp.sum(jnp.where(column_of == k, paired, 0.0), axis=1, keepdims=True) / (slab_rows * width), tile
        )
        for k in range(experts)
    ]
    splat_rows(gram_mean, keep_gram)
    statistic = [prior_wide[k] + gram_mean[k] for k in range(experts)]
    shown = statistic[0]
    for k in range(1, experts):
        shown = jnp.where(lane == k, statistic[k], shown)
    statistic_ref[...] = shown

    ridge_term = ridge_rate * total([unit[k] * statistic[k] for k in range(experts)]) / experts
    shifted = [statistic[k] + ridge_term * unit[k] for k in range(experts)]
    start_scale = 2.5 / jnp.sqrt(total([s * s for s in shifted]))
    matrix = [start_scale * s for s in shifted]
    start_root = jnp.sqrt(jnp.sqrt(start_scale))
    root = [start_root * u for u in unit]
    for repeat in range(ITERS):
        factor = [1.25 * unit[k] - 0.25 * matrix[k] for k in range(experts)]
        splat_rows(factor, keep_factor)
        if repeat == 0:
            root = [start_root * f for f in factor]
        else:
            root = times(root, keep_factor)
        if repeat < ITERS - 1:
            splat_rows(matrix, keep_matrix)
            square = times(factor, keep_factor)
            splat_rows(square, keep_square)
            matrix = times(times(square, keep_square), keep_matrix)

    root_wide = [r.astype(jnp.bfloat16).astype(jnp.float32) for r in root]
    splat_rows(root_wide, keep_factor)
    mine = [jnp.broadcast_to(keep_factor[g, pl.ds(me, 1), :], tile)[:1] for g in range(experts)]
    spread = times(root_wide, keep_gram)
    update_energy = total([spread[k] * root_wide[k] for k in range(experts)]) / experts
    grad_energy = total([unit[k] * gram_mean[k] for k in range(experts)]) / experts
    graft = jnp.sqrt((grad_energy + energy_floor) / (update_energy + energy_floor))
    graft_ref[...] = graft
    for start in range(0, width, LANES):
        columns = slice(start, start + LANES)
        products = mine[0] * held[0, :, columns].astype(jnp.float32)
        for g in range(1, experts):
            products = products + mine[g] * held[g, :, columns].astype(jnp.float32)
        mixed_ref[:, columns] = products.astype(jnp.bfloat16)


def finish(mixed_ref, wide_ref, graft_ref, update_ref, statistic_ref):
    graft = graft_ref[:1]
    for start in range(0, mixed_ref.shape[1], LANES):
        columns = slice(start, start + LANES)
        mixed = mixed_ref[:, columns].astype(jnp.float32)
        update_ref[0, :, columns] = (graft * mixed).astype(jnp.bfloat16)
    statistic_ref[...] = wide_ref[:, : statistic_ref.shape[1]]


def gathered_body(gradient, prior_stat):
    owners = lax.axis_size("expert")
    experts = prior_stat.shape[0]
    slab_rows, width = gradient.shape[1:]
    keep = pltpu.VMEM((experts, experts, LANES), jnp.float32)
    vmem = pl.BlockSpec(memory_space=pltpu.VMEM)
    mixed, wide, graft = pl.pallas_call(
        functools.partial(kernel, owners),
        out_shape=(
            pltpu.VMEM((slab_rows, width), jnp.bfloat16),
            pltpu.VMEM((experts, LANES), jnp.float32),
            pltpu.VMEM((experts, LANES), jnp.float32),
        ),
        in_specs=[pl.BlockSpec(memory_space=pltpu.HBM)] * 2,
        out_specs=(vmem, vmem, vmem),
        scratch_shapes=[
            pltpu.VMEM((experts, slab_rows, width), jnp.bfloat16),
            keep,
            keep,
            keep,
            keep,
            pltpu.VMEM(prior_stat.shape, jnp.float32),
            pltpu.SemaphoreType.DMA,
            pltpu.SemaphoreType.DMA,
            pltpu.SemaphoreType.DMA((owners,)),
            pltpu.SemaphoreType.DMA((owners,)),
        ],
        compiler_params=pltpu.CompilerParams(
            collective_id=0, has_side_effects=True, vmem_limit_bytes=KERNEL_VMEM
        ),
        name="shampoo_step",
    )(*[pltpu.with_memory_space_constraint(x, pltpu.HBM) for x in (gradient, prior_stat)])
    return pl.pallas_call(
        finish,
        out_shape=(
            jax.ShapeDtypeStruct(gradient.shape, jnp.bfloat16),
            jax.ShapeDtypeStruct(prior_stat.shape, jnp.float32),
        ),
        in_specs=[vmem, vmem, vmem],
        out_specs=(vmem, vmem),
        compiler_params=pltpu.CompilerParams(vmem_limit_bytes=KERNEL_VMEM),
        name="finish",
    )(mixed, wide, graft)


def body(gradient, prior_stat):
    owners = lax.axis_size("expert")
    experts = prior_stat.shape[0]
    gathered_bytes = 2 * experts * gradient.shape[1] * gradient.shape[2]
    fits = gathered_bytes <= VMEM_BUDGET and experts == owners and owners == 8
    regular = gradient.shape[1] % 16 == 0 and gradient.shape[2] % LANES == 0
    if fits and regular:
        return gathered_body(gradient, prior_stat)
    return wide_body(gradient, prior_stat)


def solution(mesh):
    placed = (P(("layer", "expert"), None, None), P("layer", None))
    return jax.shard_map(
        body,
        mesh=mesh,
        in_specs=placed,
        out_specs=(P(("layer", "expert"), None, None), P("layer", None)),
        check_vma=False,
    )
```

```python
import functools

import jax
import jax.numpy as jnp
from jax import lax
from jax.experimental import pallas as pl
from jax.experimental.pallas import tpu as pltpu
from jax.sharding import PartitionSpec as P

ITERS = 5
ridge_rate = 0.001
energy_floor = 1e-06
LANES = 128
VMEM_BUDGET = 16 * 1024 * 1024
KERNEL_VMEM = 32 * 1024 * 1024


def matmul_high(left, right):
    return jnp.dot(left, right, precision=lax.Precision.HIGHEST, preferred_element_type=jnp.float32)


def inverse_root(statistic):
    count_rows = statistic.shape[0]
    identity = jnp.eye(count_rows, dtype=jnp.float32)
    ridge_term = ridge_rate * jnp.trace(statistic) / count_rows
    shifted = statistic + ridge_term * identity
    start_scale = 2.5 / jnp.sqrt(jnp.sum(shifted * shifted))
    matrix = start_scale * shifted
    root = start_scale**0.25 * identity
    for repeat in range(ITERS):
        factor = 1.25 * identity - 0.25 * matrix
        root = matmul_high(root, factor)
        square = matmul_high(factor, factor)
        matrix = matmul_high(matmul_high(square, square), matrix)
    return root


def apply_graft(mixed_bf, graft):
    fenced = lax.optimization_barrier(mixed_bf)
    return (graft * fenced.astype(jnp.float32)).astype(jnp.bfloat16)


def slice_grams(pieces):
    grams = jnp.einsum("eqrf,gqrf->eqrg", pieces, pieces, preferred_element_type=jnp.float32)
    return (pieces, grams)


def wide_body(gradient, prior_stat):
    experts = prior_stat.shape[0]
    owners = lax.axis_size("expert")
    local_experts = gradient.shape[0]
    slab_rows = gradient.shape[1]
    width = gradient.shape[2]
    entry_count = slab_rows * width
    slice_rows = slab_rows // owners
    blocked = gradient.reshape(local_experts, owners, slice_rows, width)
    regrouped, row_grams = slice_grams(
        lax.all_to_all(blocked, "expert", split_axis=1, concat_axis=0, tiled=True)
    )
    summed = lax.psum(jnp.sum(row_grams, axis=(1, 2)), "expert")
    gram_mean = summed / entry_count
    statistic = prior_stat + gram_mean
    root_bf = inverse_root(statistic).astype(jnp.bfloat16)
    flattened = regrouped.reshape(experts, -1)
    products = jnp.dot(root_bf, flattened, preferred_element_type=jnp.float32)
    mixed_bf = products.astype(jnp.bfloat16).reshape(experts, slice_rows, width)
    root_wide = root_bf.astype(jnp.float32)
    update_energy = jnp.sum(matmul_high(root_wide, gram_mean) * root_wide) / experts
    grad_energy = jnp.trace(gram_mean) / experts
    graft = jnp.sqrt((grad_energy + energy_floor) / (update_energy + energy_floor))
    grafted = apply_graft(mixed_bf, graft)
    update = lax.all_to_all(grafted, "expert", split_axis=0, concat_axis=1, tiled=True)
    return (update, statistic)


def splat_rows(columns, keep):
    for m, column in enumerate(columns):
        keep[m] = column


def entry(keep, k, m):
    return jnp.broadcast_to(keep[m, k : k + 1, :], keep.shape[1:])


def times(left, keep):
    size = len(left)
    out = []
    for m in range(size):
        terms = [left[k] * entry(keep, k, m) for k in range(size)]
        while len(terms) > 1:
            terms = [terms[i] + terms[i + 1] if i + 1 < len(terms) else terms[i] for i in range(0, len(terms), 2)]
        out.append(terms[0])
    return out


def total(tiles):
    acc = tiles[0]
    for tile in tiles[1:]:
        acc = acc + tile
    return jnp.broadcast_to(jnp.sum(acc, axis=0, keepdims=True), acc.shape)


def kernel(
    owners, gradient_ref, prior_hbm, mixed_ref, statistic_ref, graft_ref, held, keep_gram, keep_matrix, keep_factor,
    keep_square, prior_ref, local_sem, prior_sem, send_sem, recv_sem, credit,
):
    me = lax.axis_index("expert")
    experts = owners
    slab_rows, width = held.shape[1:]
    rows = experts * slab_rows
    barrier = pltpu.get_barrier_semaphore()

    def signal(semaphore, device):
        pl.semaphore_signal(semaphore, inc=1, device_id={"expert": device}, device_id_type=pl.DeviceIdType.MESH)

    for peer in range(1, owners):

        @pl.when(peer > me)
        def _():
            signal(barrier, peer)

    local = pltpu.make_async_copy(gradient_ref.at[0], held.at[me], local_sem)
    local.start()
    prior_copy = pltpu.make_async_copy(prior_hbm, prior_ref, prior_sem)
    prior_copy.start()

    @pl.when(me > 0)
    def _():
        pl.semaphore_wait(barrier, me)

    def send(owner, peer):
        return pltpu.make_async_remote_copy(
            src_ref=gradient_ref.at[0],
            dst_ref=held.at[owner],
            send_sem=send_sem.at[peer],
            recv_sem=recv_sem.at[owner],
            device_id={"expert": peer},
            device_id_type=pl.DeviceIdType.MESH,
        )

    for peer in range(owners - 1):

        @pl.when(peer < me)
        def _():
            signal(credit.at[me], peer)
            send(me, peer).start()

    for peer in range(1, owners):

        @pl.when(peer > me)
        def _():
            pl.semaphore_wait(credit.at[peer], 1)
            send(me, peer).start()

    tile = (experts, LANES)
    row = lax.broadcasted_iota(jnp.int32, tile, 0)
    lane = lax.broadcasted_iota(jnp.int32, tile, 1)
    unit = [jnp.where(row == k, 1.0, 0.0).astype(jnp.float32) for k in range(experts)]
    prior_copy.wait()
    prior_wide = [jnp.broadcast_to(prior_ref[:, k : k + 1], tile) for k in range(experts)]

    local.wait()
    for peer in range(owners):

        @pl.when(peer != me)
        def _():
            send(peer, peer).wait_recv()
            send(me, peer).wait_send()

    flat = held[...].reshape(rows, width)
    full = lax.dot_general(flat, flat, (((1,), (1,)), ((), ())), preferred_element_type=jnp.float32)
    own = lax.broadcasted_iota(jnp.int32, (rows, rows), 0) % slab_rows
    other = lax.broadcasted_iota(jnp.int32, (rows, rows), 1) % slab_rows
    diagonal = jnp.where(own == other, full, 0.0)
    paired = jnp.sum(diagonal.reshape(experts, slab_rows, rows), axis=1)
    column_of = lax.broadcasted_iota(jnp.int32, (experts, rows), 1) // slab_rows
    gram_mean = [
        jnp.broadcast_to(
            jnp.sum(jnp.where(column_of == k, paired, 0.0), axis=1, keepdims=True) / (slab_rows * width), tile
        )
        for k in range(experts)
    ]
    splat_rows(gram_mean, keep_gram)
    statistic = [prior_wide[k] + gram_mean[k] for k in range(experts)]
    shown = statistic[0]
    for k in range(1, experts):
        shown = jnp.where(lane == k, statistic[k], shown)
    statistic_ref[...] = shown

    ridge_term = ridge_rate * total([unit[k] * statistic[k] for k in range(experts)]) / experts
    shifted = [statistic[k] + ridge_term * unit[k] for k in range(experts)]
    start_scale = 2.5 / jnp.sqrt(total([s * s for s in shifted]))
    matrix = [start_scale * s for s in shifted]
    start_root = jnp.sqrt(jnp.sqrt(start_scale))
    root = [start_root * u for u in unit]
    for repeat in range(ITERS):
        factor = [1.25 * unit[k] - 0.25 * matrix[k] for k in range(experts)]
        splat_rows(factor, keep_factor)
        if repeat == 0:
            root = [start_root * f for f in factor]
        else:
            root = times(root, keep_factor)
        if repeat < ITERS - 1:
            splat_rows(matrix, keep_matrix)
            square = times(factor, keep_factor)
            splat_rows(square, keep_square)
            matrix = times(times(square, keep_square), keep_matrix)

    root_wide = [r.astype(jnp.bfloat16).astype(jnp.float32) for r in root]
    splat_rows(root_wide, keep_factor)
    mine = [jnp.broadcast_to(keep_factor[g, pl.ds(me, 1), :], tile)[:1] for g in range(experts)]
    spread = times(root_wide, keep_gram)
    update_energy = total([spread[k] * root_wide[k] for k in range(experts)]) / experts
    grad_energy = total([unit[k] * gram_mean[k] for k in range(experts)]) / experts
    graft = jnp.sqrt((grad_energy + energy_floor) / (update_energy + energy_floor))
    graft_ref[...] = graft
    for start in range(0, width, LANES):
        columns = slice(start, start + LANES)
        products = mine[0] * held[0, :, columns].astype(jnp.float32)
        for g in range(1, experts):
            products = products + mine[g] * held[g, :, columns].astype(jnp.float32)
        mixed_ref[:, columns] = products.astype(jnp.bfloat16)


def finish(mixed_ref, wide_ref, graft_ref, update_ref, statistic_ref):
    graft = graft_ref[:1]
    for start in range(0, mixed_ref.shape[1], LANES):
        columns = slice(start, start + LANES)
        mixed = mixed_ref[:, columns].astype(jnp.float32)
        update_ref[0, :, columns] = (graft * mixed).astype(jnp.bfloat16)
    statistic_ref[...] = wide_ref[:, : statistic_ref.shape[1]]


def gathered_body(gradient, prior_stat):
    owners = lax.axis_size("expert")
    experts = prior_stat.shape[0]
    slab_rows, width = gradient.shape[1:]
    keep = pltpu.VMEM((experts, experts, LANES), jnp.float32)
    vmem = pl.BlockSpec(memory_space=pltpu.VMEM)
    mixed, wide, graft = pl.pallas_call(
        functools.partial(kernel, owners),
        out_shape=(
            pltpu.VMEM((slab_rows, width), jnp.bfloat16),
            pltpu.VMEM((experts, LANES), jnp.float32),
            pltpu.VMEM((experts, LANES), jnp.float32),
        ),
        in_specs=[pl.BlockSpec(memory_space=pltpu.HBM)] * 2,
        out_specs=(vmem, vmem, vmem),
        scratch_shapes=[
            pltpu.VMEM((experts, slab_rows, width), jnp.bfloat16),
            keep,
            keep,
            keep,
            keep,
            pltpu.VMEM(prior_stat.shape, jnp.float32),
            pltpu.SemaphoreType.DMA,
            pltpu.SemaphoreType.DMA,
            pltpu.SemaphoreType.DMA((owners,)),
            pltpu.SemaphoreType.DMA((owners,)),
            pltpu.SemaphoreType.REGULAR((owners,)),
        ],
        compiler_params=pltpu.CompilerParams(
            collective_id=0, has_side_effects=True, vmem_limit_bytes=KERNEL_VMEM
        ),
        name="shampoo_step",
    )(*[pltpu.with_memory_space_constraint(x, pltpu.HBM) for x in (gradient, prior_stat)])
    return pl.pallas_call(
        finish,
        out_shape=(
            jax.ShapeDtypeStruct(gradient.shape, jnp.bfloat16),
            jax.ShapeDtypeStruct(prior_stat.shape, jnp.float32),
        ),
        in_specs=[vmem, vmem, vmem],
        out_specs=(vmem, vmem),
        compiler_params=pltpu.CompilerParams(vmem_limit_bytes=KERNEL_VMEM),
        name="finish",
    )(mixed, wide, graft)


def body(gradient, prior_stat):
    owners = lax.axis_size("expert")
    experts = prior_stat.shape[0]
    gathered_bytes = 2 * experts * gradient.shape[1] * gradient.shape[2]
    fits = gathered_bytes <= VMEM_BUDGET and experts == owners and owners == 8
    regular = gradient.shape[1] % 16 == 0 and gradient.shape[2] % LANES == 0
    if fits and regular:
        return gathered_body(gradient, prior_stat)
    return wide_body(gradient, prior_stat)


def solution(mesh):
    placed = (P(("layer", "expert"), None, None), P("layer", None))
    return jax.shard_map(
        body,
        mesh=mesh,
        in_specs=placed,
        out_specs=(P(("layer", "expert"), None, None), P("layer", None)),
        check_vma=False,
    )
```
